256 devices in a mesh: seq: 32 (over z, x), head: 8 (over y, core).
Axes of the slice: x: 4, y: 4, z: 8, core: 2. Of those that a mesh axis runs over, the one named last changes fastest.
Arguments:
- queries: bfloat16 [65536, 8192], P(('seq', 'head')), may hold values from -50 to 50
- keys: bfloat16 [65536, 1024], P(('seq', 'head')), may hold values from -6 to 6
- values: bfloat16 [65536, 1024], P(('seq', 'head')), may hold values from -15 to 15
- pattern: int32 [512, 16], replicated, may hold values from 0 to 510, as said below
- keep: int32 [512, 16], replicated, may hold values from 0 to 1, as said below
Outputs:
- attended: bfloat16 [65536, 8192], P(('seq', 'head'))
The draws below stay inside these ranges and needn't reach their ends.
Inputs may be any that keep to these rules, and one draw needn't show every extreme that they name: `pattern`: entry b of query block i's list is i - 1 for b = 0; for b >= 1 it is i - 2^b or i - 2^b with its lowest bit flipped; it is 0 wherever i < 2^b. `keep`: 0 wherever i < 2^b.
All inputs are finite; a program needn't handle non-finite values.
Results may differ from the reference program's by a relative error of at most 0.0049.
Values may be sent and summed in bfloat16 or wider, within the bound.
A program may use at most 128 MiB of HBM per device.

```python
import math
import jax
import jax.numpy as jnp
from jax import lax

QUERY_HEADS = 64
KEY_VALUE_HEADS = 8
HEAD_SIZE = 128
BLOCK_TOKENS = 128
SLOTS = 16
SEQUENCE_TOKENS = 65536
SEQUENCE_BLOCKS = 512


def key_core(key):
    random_key_folder = jax.random.fold_in(key, 11)
    unscaled_keys = jnp.clip(jax.random.normal(random_key_folder, (SEQUENCE_TOKENS, KEY_VALUE_HEADS * HEAD_SIZE), jnp.float32), -6.0, 6.0)
    return unscaled_keys


def draw_keys(key, part):
    unscaled_keys = key_core(key)
    return unscaled_keys.astype(jnp.bfloat16)


def draw_queries(key, part):
    random_key_folder = jax.random.fold_in(key, 13)
    result = jnp.clip(jax.random.normal(random_key_folder, (SEQUENCE_TOKENS, QUERY_HEADS * HEAD_SIZE), jnp.float32) * 1.5, -9.0, 9.0)
    return result.astype(jnp.bfloat16)


def draw_pattern(key, part):
    block_index = jnp.arange(SEQUENCE_BLOCKS, dtype=jnp.int32)[:, None]
    level_index = jnp.arange(SLOTS, dtype=jnp.int32)[None, :]
    step_size = jnp.power(2, level_index).astype(jnp.int32)
    base_block = block_index - step_size
    flip_bits = jax.random.randint(jax.random.fold_in(key, 21), (SEQUENCE_BLOCKS, SLOTS), 0, 2, jnp.int32)
    flip_bits = jnp.where(level_index >= 1, flip_bits, 0)
    partner = base_block + flip_bits * (1 - 2 * (base_block % 2))
    return jnp.where(block_index >= step_size, partner, 0).astype(jnp.int32)


def draw_keep(key, part):
    block_index = jnp.arange(SEQUENCE_BLOCKS, dtype=jnp.int32)[:, None]
    level_index = jnp.arange(SLOTS, dtype=jnp.int32)[None, :]
    step_size = jnp.power(2, level_index).astype(jnp.int32)
    choose = jax.random.randint(jax.random.fold_in(key, 31), (SEQUENCE_BLOCKS, SLOTS), 0, 4, jnp.int32)
    return jnp.where((block_index >= step_size) & (choose > 0), 1, 0).astype(jnp.int32)


def level_of(rng, dims, cuts, least, top_value):
    gain, own = 1.0, jax.random.fold_in(rng, 6)
    for dim, blocks in cuts:
        draws = jnp.exp(jax.random.uniform(jax.random.fold_in(own, dim), (blocks,), jnp.float32, least / len(cuts), top_value / len(cuts)))
        gain = gain * jnp.repeat(draws, dims[dim] // blocks).reshape([-1 if axis == dim else 1 for axis in range(len(dims))])
    return gain


def gaussian(rng, shape, width, bound, shards=(), held_as=jnp.bfloat16):
    drawn = width * jax.random.normal(rng, shape, jnp.float32)
    if shards:
        drawn = drawn * level_of(rng, shape, shards, -0.22, 0.18)
    return jnp.clip(drawn, -bound, bound).astype(held_as)


def setup_inputs(seed: int = 0) -> dict:
    streams_of = jax.random.split(jax.random.key(seed), 6)
    return {
        "queries": draw_queries(jax.random.fold_in(streams_of[5], 71), 0),
        "keys": draw_keys(jax.random.fold_in(streams_of[5], 71), 0),
        "values": gaussian(streams_of[2], (SEQUENCE_TOKENS, KEY_VALUE_HEADS * HEAD_SIZE), 3.0, 15.0, ((0, 256),)),
        "pattern": draw_pattern(jax.random.fold_in(streams_of[5], 71), 0),
        "keep": draw_keep(jax.random.fold_in(streams_of[5], 71), 0),
    }


def reference(queries, keys, values, pattern, keep):
    group_width = QUERY_HEADS // KEY_VALUE_HEADS
    levels = (SEQUENCE_BLOCKS - 1).bit_length()
    score_scale = 1.0 / math.sqrt(HEAD_SIZE)
    key_block_rows = keys.reshape(SEQUENCE_BLOCKS, BLOCK_TOKENS, KEY_VALUE_HEADS, HEAD_SIZE)
    value_block_rows = values.reshape(SEQUENCE_BLOCKS, BLOCK_TOKENS, KEY_VALUE_HEADS, HEAD_SIZE)
    query_block_rows = queries.reshape(SEQUENCE_BLOCKS, BLOCK_TOKENS, KEY_VALUE_HEADS, group_width, HEAD_SIZE)
    causal = jnp.arange(BLOCK_TOKENS)[:, None] >= jnp.arange(BLOCK_TOKENS)[None, :]
    diag_slot = jnp.arange(levels + 1) == 0

    def block_attend(block_index):
        slot_blocks = pattern[block_index, :levels]
        key_sets = jnp.concatenate([key_block_rows[block_index][None], key_block_rows[slot_blocks]], 0).astype(jnp.float32)
        value_sets = jnp.concatenate([value_block_rows[block_index][None], value_block_rows[slot_blocks]], 0).astype(jnp.float32)
        query_rows = query_block_rows[block_index].astype(jnp.float32)
        scores = jnp.einsum('qgrd,lpgd->grqlp', query_rows, key_sets) * score_scale
        live_slots = jnp.concatenate([jnp.ones((1,), jnp.int32), keep[block_index, :levels]]) > 0
        allowed = jnp.where(diag_slot[None, :, None], causal[:, None, :], live_slots[None, :, None])
        scores = jnp.where(allowed, scores, -1e+30)
        peak = lax.optimization_barrier(jnp.max(scores, axis=(3, 4), keepdims=True))
        expo = jnp.exp(scores - peak)
        weights = (expo / lax.optimization_barrier(jnp.sum(expo, axis=(3, 4), keepdims=True))).astype(jnp.bfloat16)
        weights = lax.optimization_barrier(weights).astype(jnp.float32)
        result = jnp.einsum('grqlp,lpgd->qgrd', weights, value_sets)
        return result.astype(jnp.bfloat16).reshape(BLOCK_TOKENS, QUERY_HEADS * HEAD_SIZE)
    gathered = lax.map(block_attend, jnp.arange(SEQUENCE_BLOCKS, dtype=jnp.int32))
    return gathered.reshape(SEQUENCE_BLOCKS * BLOCK_TOKENS, QUERY_HEADS * HEAD_SIZE)
```

```python
import functools
import math

import jax
import jax.numpy as jnp
from jax import lax
from jax.experimental import pallas as pl
from jax.experimental.pallas import tpu as pltpu
from jax.sharding import PartitionSpec as P

GROUP = 8
KV_HEADS = 8
HEAD = 128
BLOCK = 128
LEVELS = 9
UNITS = 2 * KV_HEADS
SCALE = 1.0 / math.sqrt(HEAD)
NEG = -1e30
MESH = pl.DeviceIdType.MESH

R1, R2, R4, R8, R16, R32, R64, R128, VIA = range(9)
PIECES = 4


def piece_of(pair, piece):
    return pair[piece // 2].at[pl.ds((piece % 2) * BLOCK, BLOCK)]


def kernel(comm, q_hbm, k_hbm, v_hbm, pattern_hbm, keep_hbm, out_hbm, *scratch):
    buffers = scratch[:20]
    (q, out, acc, peak, pattern, keep, choice, blind, load_sem, out_sem, send_sem, recv_sem) = scratch[20:]
    own_hbm = (k_hbm, v_hbm)
    own = (buffers[0], buffers[1])
    slots = [(buffers[2 + 2 * i], buffers[3 + 2 * i]) for i in range(9)]

    if comm:
        s, h = lax.axis_index("seq"), lax.axis_index("head")
    else:
        s, h = jnp.int32(17), jnp.int32(3)
    z, x, y, c = s // 4, s % 4, h // 2, h % 2
    me = s * 8 + h

    def at(dz=0, dx=0, dy=0, dc=0):
        return (
            ((z + dz + 8) % 8) * 4 + (x + dx + 4) % 4,
            ((y + dy + 4) % 4) * 2 + (c + dc) % 2,
        )

    row0 = (me // 4) * 8
    loads = [
        pltpu.make_async_copy(pattern_hbm.at[pl.ds(row0, 8)], pattern, load_sem.at[0]),
        pltpu.make_async_copy(keep_hbm.at[pl.ds(row0, 8)], keep, load_sem.at[1]),
        pltpu.make_async_copy(k_hbm, own[0], load_sem.at[2]),
        pltpu.make_async_copy(v_hbm, own[1], load_sem.at[3]),
        pltpu.make_async_copy(q_hbm, q, load_sem.at[4]),
    ]
    for load in loads:
        load.start()

    def remote(source, slot, piece, lane, target):
        return pltpu.make_async_remote_copy(
            src_ref=piece_of(source, piece),
            dst_ref=piece_of(slots[slot], piece),
            send_sem=send_sem.at[lane, piece],
            recv_sem=recv_sem.at[slot, piece],
            device_id=target,
            device_id_type=MESH,
        )

    def arrived(slot, piece):
        if comm:
            remote(slots[slot], slot, piece, 0, at(dz=1)).wait_recv()

    Z1, X1, Y1, C1, Z2, X2, X2B, Y2, Y2B, ZP, ZM, ZM2 = range(12)

    def send(source, slot, piece, lane, target):
        remote(source, slot, piece, lane, target).start()

    if comm:
        barrier = pltpu.get_barrier_semaphore()
        partners = [
            at(dz=1), at(dz=-1), at(dz=2), at(dz=-2), at(dx=1), at(dx=-1), at(dx=2),
            at(dy=1), at(dy=-1), at(dy=2), at(dc=1),
        ]
        for partner in partners:
            pl.semaphore_signal(barrier, inc=1, device_id=partner, device_id_type=MESH)
        pl.semaphore_wait(barrier, len(partners))

        for piece in range(PIECES):
            send(own_hbm, R32, piece, Z1, at(dz=1))

            @pl.when(x < 3)
            def _():
                send(own_hbm, R8, piece, X1, at(dx=1))

            @pl.when(y < 3)
            def _():
                send(own_hbm, R2, piece, Y1, at(dy=1))

            @pl.when(c == 0)
            def _():
                send(own_hbm, R1, piece, C1, at(dc=1))

            if piece >= 2:
                send(own_hbm, VIA, piece, ZM, at(dz=-2))

    for load in loads:
        load.wait()

    line = lax.broadcasted_iota(jnp.int32, pattern.shape, 0)
    column = lax.broadcasted_iota(jnp.int32, pattern.shape, 1)
    blocks, kept = pattern[...].astype(jnp.float32), keep[...].astype(jnp.float32)
    for j in range(2):
        for level in range(LEVELS):
            here = (line == (me % 4) * 2 + j) & (column == level)

            def entry(table):
                found = jnp.where(here, table, 0.0)
                return jnp.sum(jnp.sum(found, axis=1, keepdims=True), axis=0, keepdims=True)

            if level >= 1:
                base = (2 * (me - 2 ** (level - 1))).astype(jnp.float32)
                block = jnp.clip(entry(blocks) - base, 0.0, 1.0)
                choice[j * LEVELS + level] = jnp.broadcast_to(block, (BLOCK, HEAD)).astype(jnp.bfloat16)
            blind[j * LEVELS + level] = jnp.broadcast_to((entry(kept) - 1.0) * -NEG, (8, HEAD))

    def attend(j_g, sources, first=False, last=False):
        j, g = j_g
        unit = j * KV_HEADS + g
        rows = pl.ds(pl.multiple_of(j * BLOCK, BLOCK), BLOCK)
        kv_columns = pl.ds(pl.multiple_of(g * HEAD, HEAD), HEAD)
        ones = jnp.ones((BLOCK, HEAD), jnp.bfloat16)
        keys, values, biases = [], [], []
        for pair, block, level in sources:
            table = j * LEVELS + level

            def taken(ref):
                if block is not None:
                    start = block * BLOCK
                    if not isinstance(block, int):
                        start = pl.multiple_of(start, BLOCK)
                    return ref[pl.ds(start, BLOCK), kv_columns]
                first_block, second_block = (
                    ref[pl.ds(i * BLOCK, BLOCK), kv_columns] for i in range(2)
                )
                second = choice[table]
                return first_block * (1 - second) + second_block * second

            keys.append(taken(pair[0]))
            values.append(jnp.concatenate([taken(pair[1]), ones], 1))
            biases.append(blind[table][:1])
        keys = jnp.concatenate(keys, 0)
        values = jnp.concatenate(values, 0)
        queries = jnp.concatenate(
            [
                q[rows, pl.ds(pl.multiple_of((g * GROUP + r) * HEAD, HEAD), HEAD)]
                for r in range(GROUP)
            ],
            0,
        )
        scores = lax.dot_general(
            queries, keys, (((1,), (1,)), ((), ())), preferred_element_type=jnp.float32
        )
        parts = []
        for i, bias in enumerate(biases):
            part = scores[:, i * BLOCK : (i + 1) * BLOCK]
            if first:
                token = lax.broadcasted_iota(jnp.int32, part.shape, 0) % BLOCK
                key = lax.broadcasted_iota(jnp.int32, part.shape, 1)
                part = jnp.where(key <= token, part, NEG)
            else:
                part = part + bias
            parts.append(part)
        top = functools.reduce(jnp.maximum, parts)
        top = jnp.max(top, axis=1, keepdims=True)
        top = jnp.broadcast_to(top, (GROUP * BLOCK, HEAD))
        if not first:
            before = peak[unit]
            top = jnp.maximum(before, top)
        weights = [jnp.exp((part - top) * SCALE).astype(jnp.bfloat16) for part in parts]
        weights = jnp.concatenate(weights, 1) if len(weights) > 1 else weights[0]
        total = jnp.dot(weights, values, preferred_element_type=jnp.float32)
        if not first:
            fade = jnp.exp((before - top) * SCALE)
            total = total + acc[unit] * jnp.concatenate([fade, fade], 1)
        if last:
            result = (total[:, :HEAD] / total[:, HEAD:]).astype(jnp.bfloat16)
            for r in range(GROUP):
                columns = pl.ds(pl.multiple_of((g * GROUP + r) * HEAD, HEAD), HEAD)
                out[rows, columns] = result[r * BLOCK : (r + 1) * BLOCK]
        else:
            acc[unit] = total
            peak[unit] = top

    def sweep(sources_of, first=False, last=False):
        def step(unit, carry):
            j, g = unit // KV_HEADS, unit % KV_HEADS
            attend((j, g), sources_of(j), first, last)
            if last:
                columns = pl.ds(pl.multiple_of(g * GROUP * HEAD, HEAD), GROUP * HEAD)
                rows = pl.ds(pl.multiple_of(j * BLOCK, BLOCK), BLOCK)
                pltpu.make_async_copy(
                    out.at[rows, columns], out_hbm.at[rows, columns], out_sem.at[unit]
                ).start()
            return carry

        lax.fori_loop(0, UNITS, step, 0)

    def level_source(level, slot):
        return lambda j: (slots[slot], None, level)

    sweep(lambda j: [(own, j, 0)], first=True)

    for piece in range(PIECES):
        arrived(R32, piece)
        if comm:
            send(slots[R32], R64, piece, Z2, at(dz=1))

            @pl.when(x == 3)
            def _():
                send(slots[R32], R8, piece, X1, at(dx=1))

            @pl.when(x == 2)
            def _():
                send(slots[R32], R16, piece, X2B, at(dx=2))

        arrived(R8, piece)
        if comm:

            @pl.when(x < 3)
            def _():
                send(slots[R8], R16, piece, X2, at(dx=1))

            @pl.when(y == 3)
            def _():
                send(slots[R8], R2, piece, Y1, at(dy=1))

            @pl.when(y == 2)
            def _():
                send(slots[R8], R4, piece, Y2B, at(dy=2))

        arrived(R2, piece)
        if comm:

            @pl.when(y < 3)
            def _():
                send(slots[R2], R4, piece, Y2, at(dy=1))

            @pl.when(c == 1)
            def _():
                send(slots[R2], R1, piece, C1, at(dc=1))

    for piece in (2, 3):
        arrived(VIA, piece)
        if comm:
            send(slots[VIA], R128, piece, ZM2, at(dz=-2))

    level2, level4 = level_source(2, R2), level_source(4, R8)
    level6, level3 = level_source(6, R32), level_source(3, R4)
    level5, level7 = level_source(5, R16), level_source(7, R64)
    level8 = level_source(8, R128)
    sweep(lambda j: [level6(j), level4(j)])

    for piece in (0, 1):
        arrived(R64, piece)
        if comm:
            send(slots[R64], R128, piece, ZP, at(dz=2))

    for piece in range(PIECES):
        arrived(R1, piece)
    level1 = level_source(1, R1)

    def near_sweep(j):
        def step(g, carry):
            source = (slots[R1], 1, 0) if j == 0 else (own, 0, 0)
            attend((j, g), [source, level1(j), level2(j)])
            return carry

        lax.fori_loop(0, KV_HEADS, step, 0)

    near_sweep(0)
    near_sweep(1)

    for piece in (2, 3):
        arrived(R64, piece)
    for piece in range(PIECES):
        arrived(R16, piece)
        arrived(R4, piece)
    sweep(lambda j: [level7(j), level5(j), level3(j)])

    for piece in range(PIECES):
        arrived(R128, piece)
    sweep(lambda j: [level8(j)], last=True)

    def drain(unit, carry):
        j, g = unit // KV_HEADS, unit % KV_HEADS
        columns = pl.ds(pl.multiple_of(g * GROUP * HEAD, HEAD), GROUP * HEAD)
        rows = pl.ds(pl.multiple_of(j * BLOCK, BLOCK), BLOCK)
        pltpu.make_async_copy(
            out.at[rows, columns], out_hbm.at[rows, columns], out_sem.at[unit]
        ).wait()
        return carry

    lax.fori_loop(0, UNITS, drain, 0)

    if comm:

        def sent(lane, piece):
            remote(own, R1, piece, lane, at(dz=1)).wait_send()

        for piece in range(PIECES):
            for lane in (Z1, X1, Y1, C1, Z2):
                sent(lane, piece)

            @pl.when(x < 3)
            def _():
                sent(X2, piece)

            @pl.when(x == 2)
            def _():
                sent(X2B, piece)

            @pl.when(y < 3)
            def _():
                sent(Y2, piece)

            @pl.when(y == 2)
            def _():
                sent(Y2B, piece)

            if piece < 2:
                sent(ZP, piece)
            else:
                sent(ZM, piece)
                sent(ZM2, piece)


def body(queries, keys, values, pattern, keep, comm=True):
    rows, width = queries.shape
    kv = pltpu.VMEM(keys.shape, keys.dtype)
    return pl.pallas_call(
        functools.partial(kernel, comm),
        out_shape=jax.ShapeDtypeStruct((rows, width), queries.dtype),
        in_specs=[pl.BlockSpec(memory_space=pl.ANY)] * 5,
        out_specs=pl.BlockSpec(memory_space=pl.ANY),
        scratch_shapes=[kv] * 20
        + [
            pltpu.VMEM((rows, width), queries.dtype),
            pltpu.VMEM((rows, width), queries.dtype),
            pltpu.VMEM((UNITS, GROUP * BLOCK, 2 * HEAD), jnp.float32),
            pltpu.VMEM((UNITS, GROUP * BLOCK, HEAD), jnp.float32),
            pltpu.VMEM((8, pattern.shape[1]), jnp.int32),
            pltpu.VMEM((8, keep.shape[1]), jnp.int32),
            pltpu.VMEM((2 * LEVELS, BLOCK, HEAD), jnp.bfloat16),
            pltpu.VMEM((2 * LEVELS, 8, HEAD), jnp.float32),
            pltpu.SemaphoreType.DMA((5,)),
            pltpu.SemaphoreType.DMA((UNITS,)),
            pltpu.SemaphoreType.DMA((12, PIECES)),
            pltpu.SemaphoreType.DMA((9, PIECES)),
        ],
        compiler_params=pltpu.CompilerParams(
            vmem_limit_bytes=63 * 1024 * 1024,
            **(dict(collective_id=0, has_side_effects=True) if comm else {}),
        ),
        name="butterfly_attention",
    )(queries, keys, values, pattern, keep)


def solution(mesh):
    return jax.shard_map(
        body,
        mesh=mesh,
        in_specs=(
            P(("seq", "head"), None),
            P(("seq", "head"), None),
            P(("seq", "head"), None),
            P(),
            P(),
        ),
        out_specs=P(("seq", "head"), None),
        check_vma=False,
    )
```

```python
import functools
import math

import jax
import jax.numpy as jnp
from jax import lax
from jax.experimental import pallas as pl
from jax.experimental.pallas import tpu as pltpu
from jax.sharding import PartitionSpec as P

GROUP = 8
KV_HEADS = 8
HEAD = 128
BLOCK = 128
LEVELS = 9
STEEP = math.log2(math.e) / math.sqrt(HEAD)
TILE = 8
WIDE = 2
NEG = -1e30
MESH = pl.DeviceIdType.MESH

R1, R2, R4, R8, R16, R32, R64, R128, VIA_Z, VIA_X, VIA_Y = range(11)
SLOTS = 11
PIECES = 4
HALF = KV_HEADS // 2


def piece_of(pair, which, half, rows=(0, 2 * BLOCK)):
    columns = pl.ds(pl.multiple_of(half * HALF * HEAD, HALF * HEAD), HALF * HEAD)
    return pair[which].at[pl.ds(rows[0], rows[1]), columns]


UPPER, LOWER = (0, BLOCK), (BLOCK, BLOCK)


def kernel(comm, q_hbm, k_hbm, v_hbm, pattern_hbm, keep_hbm, out_hbm, *scratch):
    buffers = scratch[: 2 * SLOTS + 2]
    (q, q_rest, out, acc, mass, peak, pattern, keep, choice, blind, load_sem, out_sem, send_sem, recv_sem) = scratch[2 * SLOTS + 2 :]
    own_hbm = (k_hbm, v_hbm)
    own = (buffers[0], buffers[1])
    slots = [(buffers[2 + 2 * i], buffers[3 + 2 * i]) for i in range(SLOTS)]

    if comm:
        s, h = lax.axis_index("seq"), lax.axis_index("head")
    else:
        s, h = jnp.int32(17), jnp.int32(3)
    z, x, y, c = s // 4, s % 4, h // 2, h % 2
    me = s * 8 + h

    def at(dz=0, dx=0, dy=0, dc=0):
        return (
            ((z + dz + 8) % 8) * 4 + (x + dx + 4) % 4,
            ((y + dy + 4) % 4) * 2 + (c + dc) % 2,
        )

    lanes = pl.ds(pl.multiple_of((me // 64) * HEAD, HEAD), HEAD)
    loads = [
        pltpu.make_async_copy(pattern_hbm.at[:, lanes], pattern, load_sem.at[0]),
        pltpu.make_async_copy(keep_hbm.at[:, lanes], keep, load_sem.at[1]),
        pltpu.make_async_copy(k_hbm, own[0], load_sem.at[2]),
        pltpu.make_async_copy(v_hbm, own[1], load_sem.at[3]),
        pltpu.make_async_copy(q_hbm, q, load_sem.at[4]),
    ]
    for load in loads:
        load.start()

    def remote(source, slot, which, half, lane, target, rows=(0, 2 * BLOCK), sem=None):
        piece = 2 * half + which if sem is None else sem
        return pltpu.make_async_remote_copy(
            src_ref=piece_of(source, which, half, rows),
            dst_ref=piece_of(slots[slot], which, half, rows),
            send_sem=send_sem.at[lane, piece],
            recv_sem=recv_sem.at[slot, piece],
            device_id=target,
            device_id_type=MESH,
        )

    def arrived(slot, which, half, rows=(0, 2 * BLOCK), sem=None):
        if comm:
            remote(slots[slot], slot, which, half, 0, at(dz=1), rows, sem).wait_recv()

    Z1, X1, Y1, C1, Z2, X2, XB, XB2, Y2, YB, YB2, ZP, ZM, ZM2 = range(14)

    def send(*args, **kwargs):
        if comm:
            remote(*args, **kwargs).start()

    def where(condition, do):
        if comm:
            pl.when(condition)(do)

    if comm:
        barrier = pltpu.get_barrier_semaphore()
        partners = [
            at(dz=1), at(dz=-1), at(dz=2), at(dz=-2), at(dx=1), at(dx=-1), at(dy=1), at(dy=-1), at(dc=1),
        ]
        for partner in partners:
            pl.semaphore_signal(barrier, inc=1, device_id=partner, device_id_type=MESH)
        pl.semaphore_wait(barrier, len(partners))

        for half in range(2):
            for which in range(2):
                send(own_hbm, R32, which, half, Z1, at(dz=1))
                where(x < 3, lambda: send(own_hbm, R8, which, half, X1, at(dx=1)))
                where(y < 3, lambda: send(own_hbm, R2, which, half, Y1, at(dy=1)))
                where(c == 0, lambda: send(own_hbm, R1, which, half, C1, at(dc=1)))
                if which == 1:
                    send(own_hbm, VIA_Z, 1, half, ZM, at(dz=-2))
        send(own_hbm, VIA_Z, 0, 1, ZM, at(dz=-2), LOWER)

    for load in loads:
        load.wait()

    line = lax.broadcasted_iota(jnp.int32, pattern.shape, 0)
    column = lax.broadcasted_iota(jnp.int32, pattern.shape, 1)
    blocks, kept = pattern[...].astype(jnp.float32), keep[...].astype(jnp.float32)
    for j in range(2):
        for level in range(LEVELS):
            here = (line == level) & (column == (me % 64) * 2 + j)

            def entry(table):
                found = jnp.where(here, table, 0.0)
                return jnp.sum(jnp.sum(found, axis=1, keepdims=True), axis=0, keepdims=True)

            if level >= 1:
                base = (2 * (me - 2 ** (level - 1))).astype(jnp.float32)
                block = jnp.clip(entry(blocks) - base, 0.0, 1.0)
                choice[j * LEVELS + level] = jnp.broadcast_to(block, (BLOCK, HEAD)).astype(jnp.bfloat16)
            blind[j * LEVELS + level] = jnp.broadcast_to((entry(kept) - 1.0) * -NEG, (8, HEAD))

    def queries_of(item, first):
        j, g, t = item
        rows = pl.ds(j * BLOCK, BLOCK)
        found = []
        for r in range(TILE):
            columns = pl.ds(pl.multiple_of((g * GROUP + t * TILE + r) * HEAD, HEAD), HEAD)
            if first:
                scaled = q[rows, columns].astype(jnp.float32) * STEEP
                whole = scaled.astype(jnp.bfloat16)
                rest = (scaled - whole.astype(jnp.float32)).astype(jnp.bfloat16)
                q[rows, columns], q_rest[rows, columns] = whole, rest
            else:
                whole, rest = q[rows, columns], q_rest[rows, columns]
            found.append(jnp.concatenate([whole, rest], 1))
        return jnp.concatenate(found, 0) if TILE > 1 else found[0]

    def gathered(j, g, sources):
        columns = pl.ds(pl.multiple_of(g * HEAD, HEAD), HEAD)

        def taken(ref, block, level):
            if block is not None:
                return ref[pl.ds(block * BLOCK, BLOCK), columns]
            first_block, second_block = (ref[pl.ds(i * BLOCK, BLOCK), columns] for i in range(2))
            second = choice[j * LEVELS + level]
            return first_block * (1 - second) + second_block * second

        keys, values = (
            [taken(pair[i], block, level) for pair, block, level in sources] for i in range(2)
        )
        keys = jnp.concatenate(keys, 0) if len(keys) > 1 else keys[0]
        values = jnp.concatenate(values, 0) if len(values) > 1 else values[0]
        return jnp.concatenate([keys, keys], 1), values

    def scores_of(item, keys, first):
        return lax.dot_general(
            queries_of(item, first), keys, (((1,), (1,)), ((), ())),
            preferred_element_type=jnp.float32,
        )

    def finish(item, scores, values, levels, first, last):
        j, g, t = item
        unit = g * 2 + j
        tile = pl.ds(t * TILE * BLOCK, TILE * BLOCK)
        parts = []
        for i, level in enumerate(levels):
            part = scores[:, i * BLOCK : (i + 1) * BLOCK]
            if first:
                token = lax.broadcasted_iota(jnp.int32, part.shape, 0) % BLOCK
                key = lax.broadcasted_iota(jnp.int32, part.shape, 1)
                part = jnp.where(key <= token, part, NEG)
            else:
                part = part + blind[j * LEVELS + level][:1]
            parts.append(part)
        top = functools.reduce(jnp.maximum, parts)
        top = jnp.max(top, axis=1, keepdims=True)
        top = jnp.broadcast_to(top, (TILE * BLOCK, HEAD))
        if not first:
            before = peak[unit, tile]
            top = jnp.maximum(before, top)
        weights = [jnp.exp2(part - top) for part in parts]
        added = functools.reduce(jnp.add, weights)
        weights = [weight.astype(jnp.bfloat16) for weight in weights]
        weights = jnp.concatenate(weights, 1) if len(weights) > 1 else weights[0]
        total = jnp.dot(weights, values, preferred_element_type=jnp.float32)
        if not first:
            fade = jnp.exp2(before - top)
            total = total + acc[unit, tile] * fade
            added = added + mass[unit, tile] * fade
        if last:
            result = (total / jnp.sum(added, axis=1, keepdims=True)).astype(jnp.bfloat16)
            for r in range(TILE):
                columns = pl.ds(pl.multiple_of((g * GROUP + t * TILE + r) * HEAD, HEAD), HEAD)
                out[pl.ds(j * BLOCK, BLOCK), columns] = result[r * BLOCK : (r + 1) * BLOCK]
        else:
            acc[unit, tile] = total
            mass[unit, tile] = added
            peak[unit, tile] = top

    def out_copy(g):
        columns = pl.ds(pl.multiple_of(g * GROUP * HEAD, HEAD), GROUP * HEAD)
        return pltpu.make_async_copy(out.at[:, columns], out_hbm.at[:, columns], out_sem.at[g])

    def sweep(half, sources_of, first=False, last=False):
        def step(i, carry):
            waiting = None
            for g in range(WIDE):
                g = half * HALF + i * WIDE + g
                for j in range(2):
                    sources = sources_of(j)
                    keys, values = gathered(j, g, sources)
                    levels = [level for _, _, level in sources]
                    for t in range(GROUP // TILE):
                        item = (j, g, t)
                        scores = scores_of(item, keys, first)
                        if waiting is not None:
                            finish(*waiting, first, last)
                        waiting = (item, scores, values, levels)
            finish(*waiting, first, last)
            if last:
                for g in range(WIDE):
                    out_copy(half * HALF + i * WIDE + g).start()
            return carry

        lax.fori_loop(0, HALF // WIDE, step, 0)

    def level_source(level, slot):
        return lambda j: (slots[slot], None, level)

    level1, level2 = level_source(1, R1), level_source(2, R2)
    level3, level4 = level_source(3, R4), level_source(4, R8)
    level5, level6 = level_source(5, R16), level_source(6, R32)
    level7, level8 = level_source(7, R64), level_source(8, R128)

    def level0(j):
        return (slots[R1], 1, 0) if j == 0 else (own, 0, 0)

    def halves(phase):
        def step(half, carry):
            phase(half)
            return carry

        lax.fori_loop(0, 2, step, 0)

    halves(lambda half: sweep(half, lambda j: [(own, j, 0)], first=True))

    def phase1(half):
        for which in range(2):
            arrived(R32, which, half)
            send(slots[R32], R64, which, half, Z2, at(dz=1))
            where(x == 3, lambda: send(slots[R32], R8, which, half, X1, at(dx=1)))
            where(x == 2, lambda: send(slots[R32], VIA_X, which, half, XB, at(dx=-1)))
            arrived(R8, which, half)
            where(x < 3, lambda: send(slots[R8], R16, which, half, X2, at(dx=1)))
            where(y == 3, lambda: send(slots[R8], R2, which, half, Y1, at(dy=1)))
            where(y == 2, lambda: send(slots[R8], VIA_Y, which, half, YB, at(dy=-1)))
        arrived(VIA_Z, 1, half)
        send(slots[VIA_Z], R128, 1, half, ZM2, at(dz=-2))
        sweep(half, lambda j: [level6(j), level4(j)])
        for which in range(2):

            def pass_x():
                arrived(VIA_X, which, half)
                send(slots[VIA_X], R16, which, half, XB2, at(dx=-1))

            where(x == 1, pass_x)
            arrived(R2, which, half)
            where(y < 3, lambda: send(slots[R2], R4, which, half, Y2, at(dy=1)))
            where(c == 1, lambda: send(slots[R2], R1, which, half, C1, at(dc=1)))

            def pass_y():
                arrived(VIA_Y, which, half)
                send(slots[VIA_Y], R4, which, half, YB2, at(dy=-1))

            where(y == 1, pass_y)

    halves(phase1)
    arrived(VIA_Z, 0, 1, LOWER)
    send(slots[VIA_Z], R128, 0, 1, ZM2, at(dz=-2), LOWER, 4)

    def near(half):
        for which in range(2):
            arrived(R1, which, half)
        sweep(half, lambda j: [level1(j), level2(j)])

    near(0)
    arrived(R64, 0, 0)
    send(slots[R64], R128, 0, 0, ZP, at(dz=2))
    near(1)
    arrived(R64, 0, 1)
    send(slots[R64], R128, 0, 1, ZP, at(dz=2), UPPER, 2)

    def phase3(half):
        arrived(R64, 1, half)
        for which in range(2):
            arrived(R16, which, half)
        sweep(half, lambda j: [level7(j), level5(j)])

    halves(phase3)

    def phase4(half):
        for which in range(2):
            arrived(R4, which, half)
        sweep(half, lambda j: [level0(j), level3(j)])

    halves(phase4)

    arrived(R128, 0, 0)
    arrived(R128, 1, 0)
    sweep(0, lambda j: [level8(j)], last=True)
    arrived(R128, 0, 1, UPPER, 2)
    arrived(R128, 0, 1, LOWER, 4)
    arrived(R128, 1, 1)
    sweep(1, lambda j: [level8(j)], last=True)

    for g in range(KV_HEADS):
        out_copy(g).wait()

    if comm:

        def sent(lane, which, half, rows=(0, 2 * BLOCK), sem=None):
            remote(own, R1, which, half, lane, at(dz=1), rows, sem).wait_send()

        for half in range(2):
            for which in range(2):
                for lane in (Z1, X1, Y1, C1, Z2):
                    sent(lane, which, half)
                for condition, lane in (
                    (x < 3, X2), (x == 2, XB), (x == 1, XB2), (y < 3, Y2), (y == 2, YB), (y == 1, YB2),
                ):
                    where(condition, lambda: sent(lane, which, half))
            sent(ZM, 1, half)
            sent(ZM2, 1, half)
        sent(ZM, 0, 1, LOWER)
        sent(ZM2, 0, 1, LOWER, 4)
        sent(ZP, 0, 0)
        sent(ZP, 0, 1, UPPER, 2)


def body(queries, keys, values, pattern, keep, comm=True):
    rows, width = queries.shape
    kv = pltpu.VMEM(keys.shape, keys.dtype)
    return pl.pallas_call(
        functools.partial(kernel, comm),
        out_shape=jax.ShapeDtypeStruct((rows, width), queries.dtype),
        in_specs=[pl.BlockSpec(memory_space=pl.ANY)] * 5,
        out_specs=pl.BlockSpec(memory_space=pl.ANY),
        scratch_shapes=[kv] * (2 * SLOTS + 2)
        + [
            pltpu.VMEM((rows, width), queries.dtype),
            pltpu.VMEM((rows, width), queries.dtype),
            pltpu.VMEM((rows, width), queries.dtype),
            pltpu.VMEM((2 * KV_HEADS, GROUP * BLOCK, HEAD), jnp.float32),
            pltpu.VMEM((2 * KV_HEADS, GROUP * BLOCK, HEAD), jnp.float32),
            pltpu.VMEM((2 * KV_HEADS, GROUP * BLOCK, HEAD), jnp.float32),
            pltpu.VMEM((pattern.shape[1], HEAD), jnp.int32),
            pltpu.VMEM((keep.shape[1], HEAD), jnp.int32),
            pltpu.VMEM((2 * LEVELS, BLOCK, HEAD), jnp.bfloat16),
            pltpu.VMEM((2 * LEVELS, 8, HEAD), jnp.float32),
            pltpu.SemaphoreType.DMA((5,)),
            pltpu.SemaphoreType.DMA((KV_HEADS,)),
            pltpu.SemaphoreType.DMA((14, PIECES + 1)),
            pltpu.SemaphoreType.DMA((SLOTS, PIECES + 1)),
        ],
        compiler_params=pltpu.CompilerParams(
            vmem_limit_bytes=63 * 1024 * 1024,
            **(dict(collective_id=0, has_side_effects=True) if comm else {}),
        ),
        name="butterfly_attention",
    )(queries, keys, values, pattern.T, keep.T)


def solution(mesh):
    return jax.shard_map(
        body,
        mesh=mesh,
        in_specs=(
            P(("seq", "head"), None),
            P(("seq", "head"), None),
            P(("seq", "head"), None),
            P(),
            P(),
        ),
        out_specs=P(("seq", "head"), None),
        check_vma=False,
    )
```

```python
import functools
import math

import jax
import jax.numpy as jnp
from jax import lax
from jax.experimental import pallas as pl
from jax.experimental.pallas import tpu as pltpu
from jax.sharding import PartitionSpec as P

GROUP = 8
KV_HEADS = 8
HEAD = 128
BLOCK = 128
LEVELS = 9
STEEP = math.log2(math.e) / math.sqrt(HEAD)
TILE = 8
WIDE = 2
NEG = -1e30
MESH = pl.DeviceIdType.MESH

R1, R2, R4, R8, R16, R32, R64, R128, VIA_Z, VIA_X, VIA_Y = range(11)
SLOTS = 11
PIECES = 4
HALF = KV_HEADS // 2


def piece_of(pair, which, half, rows=(0, 2 * BLOCK)):
    columns = pl.ds(pl.multiple_of(half * HALF * HEAD, HALF * HEAD), HALF * HEAD)
    return pair[which].at[pl.ds(rows[0], rows[1]), columns]


UPPER, LOWER = (0, 208), (208, 48)


def kernel(comm, q_hbm, k_hbm, v_hbm, pattern_hbm, keep_hbm, out_hbm, *scratch):
    buffers = scratch[: 2 * SLOTS + 2]
    (q, q_rest, out, acc, peak, pattern, keep, first_table, second_table, none_table, load_sem, out_sem, send_sem, recv_sem) = scratch[2 * SLOTS + 2 :]
    own_hbm = (k_hbm, v_hbm)
    own = (buffers[0], buffers[1])
    slots = [(buffers[2 + 2 * i], buffers[3 + 2 * i]) for i in range(SLOTS)]

    if comm:
        s, h = lax.axis_index("seq"), lax.axis_index("head")
    else:
        s, h = jnp.int32(17), jnp.int32(3)
    z, x, y, c = s // 4, s % 4, h // 2, h % 2
    me = s * 8 + h

    def at(dz=0, dx=0, dy=0, dc=0):
        return (
            ((z + dz + 8) % 8) * 4 + (x + dx + 4) % 4,
            ((y + dy + 4) % 4) * 2 + (c + dc) % 2,
        )

    lanes = pl.ds(pl.multiple_of((me // 64) * HEAD, HEAD), HEAD)
    loads = [
        pltpu.make_async_copy(pattern_hbm.at[:, lanes], pattern, load_sem.at[0]),
        pltpu.make_async_copy(keep_hbm.at[:, lanes], keep, load_sem.at[1]),
        pltpu.make_async_copy(k_hbm, own[0], load_sem.at[2]),
        pltpu.make_async_copy(v_hbm, own[1], load_sem.at[3]),
        pltpu.make_async_copy(q_hbm, q, load_sem.at[4]),
    ]
    for load in loads:
        load.start()

    def remote(source, slot, which, half, lane, target, rows=(0, 2 * BLOCK), sem=None):
        piece = 2 * half + which if sem is None else sem
        return pltpu.make_async_remote_copy(
            src_ref=piece_of(source, which, half, rows),
            dst_ref=piece_of(slots[slot], which, half, rows),
            send_sem=send_sem.at[lane, piece],
            recv_sem=recv_sem.at[slot, piece],
            device_id=target,
            device_id_type=MESH,
        )

    def arrived(slot, which, half, rows=(0, 2 * BLOCK), sem=None):
        if comm:
            remote(slots[slot], slot, which, half, 0, at(dz=1), rows, sem).wait_recv()

    Z1, X1, Y1, C1, Z2, X2, XB, XB2, Y2, YB, YB2, ZP, ZM, ZM2 = range(14)

    def send(*args, **kwargs):
        if comm:
            remote(*args, **kwargs).start()

    def where(condition, do):
        if comm:
            pl.when(condition)(do)

    if comm:
        barrier = pltpu.get_barrier_semaphore()
        partners = [
            at(dz=1), at(dz=-1), at(dz=2), at(dz=-2), at(dx=1), at(dx=-1), at(dy=1), at(dy=-1), at(dc=1),
        ]
        for partner in partners:
            pl.semaphore_signal(barrier, inc=1, device_id=partner, device_id_type=MESH)
        pl.semaphore_wait(barrier, len(partners))

        for half in range(2):
            for which in range(2):
                send(own_hbm, R32, which, half, Z1, at(dz=1))
                where(x < 3, lambda: send(own_hbm, R8, which, half, X1, at(dx=1)))
                where(y < 3, lambda: send(own_hbm, R2, which, half, Y1, at(dy=1)))
                where(c == 0, lambda: send(own_hbm, R1, which, half, C1, at(dc=1)))
            send(own_hbm, VIA_Z, 1, half, ZM, at(dz=-2))
            send(own_hbm, VIA_Z, 0, half, ZM, at(dz=-2), LOWER)

    for load in loads:
        load.wait()

    line = lax.broadcasted_iota(jnp.int32, pattern.shape, 0)
    column = lax.broadcasted_iota(jnp.int32, pattern.shape, 1)
    blocks, kept = pattern[...].astype(jnp.float32), keep[...].astype(jnp.float32)
    for j in range(2):
        for level in range(LEVELS):
            here = (line == level) & (column == (me % 64) * 2 + j)

            def entry(table):
                found = jnp.where(here, table, 0.0)
                return jnp.sum(jnp.sum(found, axis=1, keepdims=True), axis=0, keepdims=True)

            base = (2 * (me - max(1, 2**level // 2))).astype(jnp.float32)
            second = jnp.clip(entry(blocks) - base, 0.0, 1.0)
            used = entry(kept)
            if level == 0:
                second = jnp.zeros_like(second)
            for table, value in (
                (first_table, used * (1.0 - second)), (second_table, used * second), (none_table, 1.0 - used),
            ):
                table[j * LEVELS + level] = jnp.broadcast_to(value, (BLOCK, HEAD)).astype(jnp.bfloat16)

    def queries_of(item, first):
        j, g, t = item
        rows = pl.ds(j * BLOCK, BLOCK)
        found = []
        for r in range(TILE):
            columns = pl.ds(pl.multiple_of((g * GROUP + t * TILE + r) * HEAD, HEAD), HEAD)
            if first:
                scaled = q[rows, columns].astype(jnp.float32) * STEEP
                whole = scaled.astype(jnp.bfloat16)
                rest = (scaled - whole.astype(jnp.float32)).astype(jnp.bfloat16)
                q[rows, columns], q_rest[rows, columns] = whole, rest
            else:
                whole, rest = q[rows, columns], q_rest[rows, columns]
            found.append(jnp.concatenate([whole, rest], 1))
        return jnp.concatenate(found, 0) if TILE > 1 else found[0]

    def gathered(j, g, sources):
        columns = pl.ds(pl.multiple_of(g * HEAD, HEAD), HEAD)

        anchor = jnp.broadcast_to(own[0][pl.ds(j * BLOCK, 1), columns], (BLOCK, HEAD))
        keys, values = [], []
        for pair, block, level in sources:
            key, value = (
                [ref[pl.ds(i * BLOCK, BLOCK), columns] for i in (range(2) if block is None else (block,))]
                for ref in pair
            )
            if level is None:
                keys.append(key[0])
                values.append(jnp.concatenate([value[0], jnp.ones_like(value[0])], 1))
                continue
            table = j * LEVELS + level
            one, none = first_table[table], none_table[table]
            total_key, total_value = key[0] * one + anchor * none, value[0] * one
            ones = one
            if block is None:
                two = second_table[table]
                total_key, total_value = total_key + key[1] * two, total_value + value[1] * two
                ones = one + two
            keys.append(total_key)
            values.append(jnp.concatenate([total_value, ones], 1))
        keys = jnp.concatenate(keys, 0) if len(keys) > 1 else keys[0]
        values = jnp.concatenate(values, 0) if len(values) > 1 else values[0]
        return jnp.concatenate([keys, keys], 1), values

    def scores_of(item, keys, first):
        return lax.dot_general(
            queries_of(item, first), keys, (((1,), (1,)), ((), ())),
            preferred_element_type=jnp.float32,
        )

    def finish(item, scores, values, levels, first, last):
        j, g, t = item
        unit = g * 2 + j
        tile = pl.ds(t * TILE * BLOCK, TILE * BLOCK)
        parts = []
        for i, level in enumerate(levels):
            part = scores[:, i * BLOCK : (i + 1) * BLOCK]
            if level is None:
                token = lax.broadcasted_iota(jnp.int32, part.shape, 0) % BLOCK
                key = lax.broadcasted_iota(jnp.int32, part.shape, 1)
                part = jnp.where(key <= token, part, NEG)
            parts.append(part)
        top = functools.reduce(jnp.maximum, parts)
        top = jnp.max(top, axis=1, keepdims=True)
        top = jnp.broadcast_to(top, (TILE * BLOCK, HEAD))
        if not first:
            before = peak[unit, tile]
            top = jnp.maximum(before, top)
        weights = [jnp.exp2(part - top).astype(jnp.bfloat16) for part in parts]
        weights = jnp.concatenate(weights, 1) if len(weights) > 1 else weights[0]
        total = jnp.dot(weights, values, preferred_element_type=jnp.float32)
        if not first:
            fade = jnp.exp2(before - top)
            total = total + acc[unit, tile] * jnp.concatenate([fade, fade], 1)
        if last:
            result = (total[:, :HEAD] / total[:, HEAD:]).astype(jnp.bfloat16)
            for r in range(TILE):
                columns = pl.ds(pl.multiple_of((g * GROUP + t * TILE + r) * HEAD, HEAD), HEAD)
                out[pl.ds(j * BLOCK, BLOCK), columns] = result[r * BLOCK : (r + 1) * BLOCK]
        else:
            acc[unit, tile] = total
            peak[unit, tile] = top

    def out_copy(g):
        columns = pl.ds(pl.multiple_of(g * GROUP * HEAD, HEAD), GROUP * HEAD)
        return pltpu.make_async_copy(out.at[:, columns], out_hbm.at[:, columns], out_sem.at[g])

    def sweep(half, sources_of, first=False, last=False):
        def step(i, carry):
            waiting = None
            for g in range(WIDE):
                g = half * HALF + i * WIDE + g
                for j in range(2):
                    sources = sources_of(j)
                    if not sources:
                        continue
                    keys, values = gathered(j, g, sources)
                    levels = [level for _, _, level in sources]
                    for t in range(GROUP // TILE):
                        item = (j, g, t)
                        scores = scores_of(item, keys, first)
                        if waiting is not None:
                            finish(*waiting, first, last)
                        waiting = (item, scores, values, levels)
            finish(*waiting, first, last)
            if last:
                for g in range(WIDE):
                    out_copy(half * HALF + i * WIDE + g).start()
            return carry

        lax.fori_loop(0, HALF // WIDE, step, 0)

    def level_source(level, slot):
        return lambda j: (slots[slot], None, level)

    level1, level2 = level_source(1, R1), level_source(2, R2)
    level3, level4 = level_source(3, R4), level_source(4, R8)
    level5, level6 = level_source(5, R16), level_source(6, R32)
    level7, level8 = level_source(7, R64), level_source(8, R128)

    def halves(phase):
        def step(half, carry):
            phase(half)
            return carry

        lax.fori_loop(0, 2, step, 0)

    def diagonal(j):
        return [(own, j, None)] + [(own, 0, 0)] * j

    halves(lambda half: sweep(half, diagonal, first=True))

    def phase1(half):
        for which in range(2):
            arrived(R32, which, half)
            send(slots[R32], R64, which, half, Z2, at(dz=1))
            where(x == 3, lambda: send(slots[R32], R8, which, half, X1, at(dx=1)))
            where(x == 2, lambda: send(slots[R32], VIA_X, which, half, XB, at(dx=-1)))
            arrived(R8, which, half)
            where(x < 3, lambda: send(slots[R8], R16, which, half, X2, at(dx=1)))
            where(y == 3, lambda: send(slots[R8], R2, which, half, Y1, at(dy=1)))
            where(y == 2, lambda: send(slots[R8], VIA_Y, which, half, YB, at(dy=-1)))
        arrived(VIA_Z, 1, half)
        send(slots[VIA_Z], R128, 1, half, ZM2, at(dz=-2))
        arrived(VIA_Z, 0, half, LOWER)
        send(slots[VIA_Z], R128, 0, half, ZM2, at(dz=-2), LOWER, 4 + half)
        sweep(half, lambda j: [level6(j), level4(j)])

    def near(half):
        for which in range(2):

            def pass_x():
                arrived(VIA_X, which, half)
                send(slots[VIA_X], R16, which, half, XB2, at(dx=-1))

            where(x == 1, pass_x)
            arrived(R2, which, half)
            where(y < 3, lambda: send(slots[R2], R4, which, half, Y2, at(dy=1)))
            where(c == 1, lambda: send(slots[R2], R1, which, half, C1, at(dc=1)))

            def pass_y():
                arrived(VIA_Y, which, half)
                send(slots[VIA_Y], R4, which, half, YB2, at(dy=-1))

            where(y == 1, pass_y)

        for which in range(2):
            arrived(R1, which, half)
        sweep(half, lambda j: [level1(j), level2(j)])

    def far(half):
        arrived(R64, 0, half)
        send(slots[R64], R128, 0, half, ZP, at(dz=2), UPPER)
        arrived(R64, 1, half)
        for which in range(2):
            arrived(R16, which, half)
        sweep(half, lambda j: [level7(j), level5(j)])

    def middle(half):
        for which in range(2):
            arrived(R4, which, half)
        sweep(half, lambda j: [] if j else [(slots[R1], 1, 0), level3(j)])

    late = jnp.where((x == 0) & (y <= 1), 1, 0) if comm else 0

    def stage(i, carry):
        pl.when(i < 2)(lambda: phase1(i))
        pl.when((i == 0) | (i == 1 + late))(lambda: near(jnp.minimum(i, 1)))
        pl.when((i == 2 - late) | (i == 3))(lambda: far(i // 3))
        pl.when(i >= 2)(lambda: middle(i - 2))
        return carry

    lax.fori_loop(0, 4, stage, 0)

    def phase3(half):
        arrived(R128, 0, half, UPPER)
        arrived(R128, 0, half, LOWER, 4 + half)
        arrived(R128, 1, half)
        sweep(half, lambda j: [level8(j)] + [level3(j)] * j, last=True)

    halves(phase3)

    for g in range(KV_HEADS):
        out_copy(g).wait()

    if comm:

        def sent(lane, which, half, rows=(0, 2 * BLOCK), sem=None):
            remote(own, R1, which, half, lane, at(dz=1), rows, sem).wait_send()

        for half in range(2):
            for which in range(2):
                for lane in (Z1, X1, Y1, C1, Z2):
                    sent(lane, which, half)
                for condition, lane in (
                    (x < 3, X2), (x == 2, XB), (x == 1, XB2), (y < 3, Y2), (y == 2, YB), (y == 1, YB2),
                ):
                    where(condition, lambda: sent(lane, which, half))
            for lane in (ZM, ZM2):
                sent(lane, 1, half)
            sent(ZM, 0, half, LOWER)
            sent(ZM2, 0, half, LOWER, 4 + half)
            sent(ZP, 0, half, UPPER)


def copy_kernel(source, target, held, in_sem, out_sem):
    chunks, rows = held.shape[0], held.shape[1]

    def read(i):
        return pltpu.make_async_copy(source.at[pl.ds(i * rows, rows)], held.at[i], in_sem.at[i])

    def write(i):
        return pltpu.make_async_copy(held.at[i], target.at[pl.ds(i * rows, rows)], out_sem.at[i])

    for i in range(chunks):
        read(i).start()
    for i in range(chunks):
        read(i).wait()
        write(i).start()
    for i in range(chunks):
        write(i).wait()


def copied(array):
    rows, width = array.shape
    chunks = 16
    return pl.pallas_call(
        copy_kernel,
        out_shape=jax.ShapeDtypeStruct(array.shape, array.dtype),
        in_specs=[pl.BlockSpec(memory_space=pl.ANY)],
        out_specs=pl.BlockSpec(memory_space=pl.ANY),
        scratch_shapes=[
            pltpu.VMEM((chunks, rows // chunks, width), array.dtype),
            pltpu.SemaphoreType.DMA((chunks,)),
            pltpu.SemaphoreType.DMA((chunks,)),
        ],
        compiler_params=pltpu.CompilerParams(vmem_limit_bytes=63 * 1024 * 1024),
        name="copy_out",
    )(array)


def body(queries, keys, values, pattern, keep, comm=True):
    rows, width = queries.shape
    kv = pltpu.VMEM(keys.shape, keys.dtype)
    result = pl.pallas_call(
        functools.partial(kernel, comm),
        out_shape=jax.ShapeDtypeStruct((rows, width), queries.dtype),
        in_specs=[pl.BlockSpec(memory_space=pl.ANY)] * 5,
        out_specs=pl.BlockSpec(memory_space=pl.ANY),
        scratch_shapes=[kv] * (2 * SLOTS + 2)
        + [
            pltpu.VMEM((rows, width), queries.dtype),
            pltpu.VMEM((rows, width), queries.dtype),
            pltpu.VMEM((rows, width), queries.dtype),
            pltpu.VMEM((2 * KV_HEADS, GROUP * BLOCK, 2 * HEAD), jnp.float32),
            pltpu.VMEM((2 * KV_HEADS, GROUP * BLOCK, HEAD), jnp.float32),
            pltpu.VMEM((pattern.shape[1], HEAD), jnp.int32),
            pltpu.VMEM((keep.shape[1], HEAD), jnp.int32),
            pltpu.VMEM((2 * LEVELS, BLOCK, HEAD), jnp.bfloat16),
            pltpu.VMEM((2 * LEVELS, BLOCK, HEAD), jnp.bfloat16),
            pltpu.VMEM((2 * LEVELS, BLOCK, HEAD), jnp.bfloat16),
            pltpu.SemaphoreType.DMA((5,)),
            pltpu.SemaphoreType.DMA((KV_HEADS,)),
            pltpu.SemaphoreType.DMA((14, PIECES + 2)),
            pltpu.SemaphoreType.DMA((SLOTS, PIECES + 2)),
        ],
        compiler_params=pltpu.CompilerParams(
            vmem_limit_bytes=63 * 1024 * 1024,
            **(dict(collective_id=0, has_side_effects=True) if comm else {}),
        ),
        name="butterfly_attention",
    )(queries, keys, values, pattern.T, keep.T)
    return copied(result)


def solution(mesh):
    return jax.shard_map(
        body,
        mesh=mesh,
        in_specs=(
            P(("seq", "head"), None),
            P(("seq", "head"), None),
            P(("seq", "head"), None),
            P(),
            P(),
        ),
        out_specs=P(("seq", "head"), None),
        check_vma=False,
    )
```

```python
import functools
import math

import jax
import jax.numpy as jnp
from jax import lax
from jax.experimental import pallas as pl
from jax.experimental.pallas import tpu as pltpu
from jax.sharding import PartitionSpec as P

GROUP = 8
KV_HEADS = 8
HEAD = 128
BLOCK = 128
LEVELS = 9
STEEP = math.log2(math.e) / math.sqrt(HEAD)
TILE = 8
WIDE = 2
NEG = -1e30
MESH = pl.DeviceIdType.MESH

R1, R2, R4, R8, R16, R32, R64, R128, VIA_Z, VIA_X, VIA_Y = range(11)
SLOTS = 11
PIECES = 4
HALF = KV_HEADS // 2


def piece_of(pair, which, half, rows=(0, 2 * BLOCK)):
    columns = pl.ds(pl.multiple_of(half * HALF * HEAD, HALF * HEAD), HALF * HEAD)
    return pair[which].at[pl.ds(rows[0], rows[1]), columns]


UPPER, LOWER = (0, 208), (208, 48)


def kernel(comm, q_hbm, k_hbm, v_hbm, pattern_hbm, keep_hbm, out_hbm, *scratch):
    buffers = scratch[: 2 * SLOTS + 2]
    (q, q_rest, out, acc, peak, pattern, keep, first_table, second_table, none_table, load_sem, out_sem, send_sem, recv_sem) = scratch[2 * SLOTS + 2 :]
    own_hbm = (k_hbm, v_hbm)
    own = (buffers[0], buffers[1])
    slots = [(buffers[2 + 2 * i], buffers[3 + 2 * i]) for i in range(SLOTS)]

    if comm:
        s, h = lax.axis_index("seq"), lax.axis_index("head")
    else:
        s, h = jnp.int32(17), jnp.int32(3)
    z, x, y, c = s // 4, s % 4, h // 2, h % 2
    me = s * 8 + h

    def at(dz=0, dx=0, dy=0, dc=0):
        return (
            ((z + dz + 8) % 8) * 4 + (x + dx + 4) % 4,
            ((y + dy + 4) % 4) * 2 + (c + dc) % 2,
        )

    lanes = pl.ds(pl.multiple_of((me // 64) * HEAD, HEAD), HEAD)
    loads = [
        pltpu.make_async_copy(pattern_hbm.at[:, lanes], pattern, load_sem.at[0]),
        pltpu.make_async_copy(keep_hbm.at[:, lanes], keep, load_sem.at[1]),
        pltpu.make_async_copy(k_hbm, own[0], load_sem.at[2]),
        pltpu.make_async_copy(v_hbm, own[1], load_sem.at[3]),
        pltpu.make_async_copy(q_hbm, q, load_sem.at[4]),
    ]
    for load in loads:
        load.start()

    def remote(source, slot, which, half, lane, target, rows=(0, 2 * BLOCK), sem=None):
        piece = 2 * half + which if sem is None else sem
        return pltpu.make_async_remote_copy(
            src_ref=piece_of(source, which, half, rows),
            dst_ref=piece_of(slots[slot], which, half, rows),
            send_sem=send_sem.at[lane, piece],
            recv_sem=recv_sem.at[slot, piece],
            device_id=target,
            device_id_type=MESH,
        )

    def arrived(slot, which, half, rows=(0, 2 * BLOCK), sem=None):
        if comm:
            remote(slots[slot], slot, which, half, 0, at(dz=1), rows, sem).wait_recv()

    Z1, X1, Y1, C1, Z2, X2, XB, XB2, Y2, YB, YB2, ZP, ZM, ZM2 = range(14)

    def send(*args, **kwargs):
        if comm:
            remote(*args, **kwargs).start()

    def where(condition, do):
        if comm:
            pl.when(condition)(do)

    if comm:
        barrier = pltpu.get_barrier_semaphore()
        partners = [
            at(dz=1), at(dz=-1), at(dz=2), at(dz=-2), at(dx=1), at(dx=-1), at(dy=1), at(dy=-1), at(dc=1),
        ]
        for partner in partners:
            pl.semaphore_signal(barrier, inc=1, device_id=partner, device_id_type=MESH)
        pl.semaphore_wait(barrier, len(partners))

        for half in range(2):
            for which in range(2):
                send(own_hbm, R32, which, half, Z1, at(dz=1))
                where(x < 3, lambda: send(own_hbm, R8, which, half, X1, at(dx=1)))
                where(y < 3, lambda: send(own_hbm, R2, which, half, Y1, at(dy=1)))
                where(c == 0, lambda: send(own_hbm, R1, which, half, C1, at(dc=1)))
            send(own_hbm, VIA_Z, 1, half, ZM, at(dz=-2))
            send(own_hbm, VIA_Z, 0, half, ZM, at(dz=-2), LOWER)

    for load in loads:
        load.wait()

    line = lax.broadcasted_iota(jnp.int32, pattern.shape, 0)
    column = lax.broadcasted_iota(jnp.int32, pattern.shape, 1)
    blocks, kept = pattern[...].astype(jnp.float32), keep[...].astype(jnp.float32)
    for j in range(2):
        for level in range(LEVELS):
            here = (line == level) & (column == (me % 64) * 2 + j)

            def entry(table):
                found = jnp.where(here, table, 0.0)
                return jnp.sum(jnp.sum(found, axis=1, keepdims=True), axis=0, keepdims=True)

            base = (2 * (me - max(1, 2**level // 2))).astype(jnp.float32)
            second = jnp.clip(entry(blocks) - base, 0.0, 1.0)
            used = entry(kept)
            if level == 0:
                second = jnp.zeros_like(second)
            for table, value in (
                (first_table, used * (1.0 - second)), (second_table, used * second), (none_table, 1.0 - used),
            ):
                table[j * LEVELS + level] = jnp.broadcast_to(value, (BLOCK, HEAD)).astype(jnp.bfloat16)

    def queries_of(item, first):
        j, g, t = item
        rows = pl.ds(j * BLOCK, BLOCK)
        found = []
        for r in range(TILE):
            columns = pl.ds(pl.multiple_of((g * GROUP + t * TILE + r) * HEAD, HEAD), HEAD)
            if first:
                scaled = q[rows, columns].astype(jnp.float32) * STEEP
                whole = scaled.astype(jnp.bfloat16)
                rest = (scaled - whole.astype(jnp.float32)).astype(jnp.bfloat16)
                q[rows, columns], q_rest[rows, columns] = whole, rest
            else:
                whole, rest = q[rows, columns], q_rest[rows, columns]
            found.append(jnp.concatenate([whole, rest], 1))
        return jnp.concatenate(found, 0) if TILE > 1 else found[0]

    def gathered(j, g, sources):
        columns = pl.ds(pl.multiple_of(g * HEAD, HEAD), HEAD)

        anchor = jnp.broadcast_to(own[0][pl.ds(j * BLOCK, 1), columns], (BLOCK, HEAD))
        keys, values = [], []
        for pair, block, level in sources:
            key, value = (
                [ref[pl.ds(i * BLOCK, BLOCK), columns] for i in (range(2) if block is None else (block,))]
                for ref in pair
            )
            if level is None:
                keys.append(key[0])
                values.append(jnp.concatenate([value[0], jnp.ones_like(value[0])], 1))
                continue
            table = j * LEVELS + level
            one, none = first_table[table], none_table[table]
            total_key, total_value = key[0] * one + anchor * none, value[0] * one
            ones = one
            if block is None:
                two = second_table[table]
                total_key, total_value = total_key + key[1] * two, total_value + value[1] * two
                ones = one + two
            keys.append(total_key)
            values.append(jnp.concatenate([total_value, ones], 1))
        keys = jnp.concatenate(keys, 0) if len(keys) > 1 else keys[0]
        values = jnp.concatenate(values, 0) if len(values) > 1 else values[0]
        return jnp.concatenate([keys, keys], 1), values

    def scores_of(item, keys, first):
        return lax.dot_general(
            queries_of(item, first), keys, (((1,), (1,)), ((), ())),
            preferred_element_type=jnp.float32,
        )

    def finish(item, scores, values, levels, first, last):
        j, g, t = item
        unit = g * 2 + j
        tile = pl.ds(t * TILE * BLOCK, TILE * BLOCK)
        parts = []
        for i, level in enumerate(levels):
            part = scores[:, i * BLOCK : (i + 1) * BLOCK]
            if level is None:
                token = lax.broadcasted_iota(jnp.int32, part.shape, 0) % BLOCK
                key = lax.broadcasted_iota(jnp.int32, part.shape, 1)
                part = jnp.where(key <= token, part, NEG)
            parts.append(part)
        top = functools.reduce(jnp.maximum, parts)
        top = jnp.max(top, axis=1, keepdims=True)
        top = jnp.broadcast_to(top, (TILE * BLOCK, HEAD))
        if not first:
            before = peak[unit, tile]
            top = jnp.maximum(before, top)
        weights = [jnp.exp2(part - top).astype(jnp.bfloat16) for part in parts]
        weights = jnp.concatenate(weights, 1) if len(weights) > 1 else weights[0]
        total = jnp.dot(weights, values, preferred_element_type=jnp.float32)
        if not first:
            fade = jnp.exp2(before - top)
            total = total + acc[unit, tile] * jnp.concatenate([fade, fade], 1)
        if last:
            result = (total[:, :HEAD] / total[:, HEAD:]).astype(jnp.bfloat16)
            for r in range(TILE):
                columns = pl.ds(pl.multiple_of((g * GROUP + t * TILE + r) * HEAD, HEAD), HEAD)
                out[pl.ds(j * BLOCK, BLOCK), columns] = result[r * BLOCK : (r + 1) * BLOCK]
        else:
            acc[unit, tile] = total
            peak[unit, tile] = top

    def out_copy(g):
        columns = pl.ds(pl.multiple_of(g * GROUP * HEAD, HEAD), GROUP * HEAD)
        return pltpu.make_async_copy(out.at[:, columns], out_hbm.at[:, columns], out_sem.at[g])

    def sweep(half, sources_of, first=False, last=False):
        def step(i, carry):
            waiting = None
            for g in range(WIDE):
                g = half * HALF + i * WIDE + g
                for j in range(2):
                    sources = sources_of(j)
                    if not sources:
                        continue
                    keys, values = gathered(j, g, sources)
                    levels = [level for _, _, level in sources]
                    for t in range(GROUP // TILE):
                        item = (j, g, t)
                        scores = scores_of(item, keys, first)
                        if waiting is not None:
                            finish(*waiting, first, last)
                        waiting = (item, scores, values, levels)
            finish(*waiting, first, last)
            if last:
                for g in range(WIDE):
                    out_copy(half * HALF + i * WIDE + g).start()
            return carry

        lax.fori_loop(0, HALF // WIDE, step, 0)

    def level_source(level, slot):
        return lambda j: (slots[slot], None, level)

    level1, level2 = level_source(1, R1), level_source(2, R2)
    level3, level4 = level_source(3, R4), level_source(4, R8)
    level5, level6 = level_source(5, R16), level_source(6, R32)
    level7, level8 = level_source(7, R64), level_source(8, R128)

    def halves(phase):
        def step(half, carry):
            phase(half)
            return carry

        lax.fori_loop(0, 2, step, 0)

    def diagonal(j):
        return [(own, j, None)] + [(own, 0, 0)] * j

    halves(lambda half: sweep(half, diagonal, first=True))

    def phase1(half):
        for which in range(2):
            arrived(R32, which, half)
            send(slots[R32], R64, which, half, Z2, at(dz=1))
            where(x == 3, lambda: send(slots[R32], R8, which, half, X1, at(dx=1)))
            where(x == 2, lambda: send(slots[R32], VIA_X, which, half, XB, at(dx=-1)))
            arrived(R8, which, half)
            where(x < 3, lambda: send(slots[R8], R16, which, half, X2, at(dx=1)))
            where(y == 3, lambda: send(slots[R8], R2, which, half, Y1, at(dy=1)))
            where(y == 2, lambda: send(slots[R8], VIA_Y, which, half, YB, at(dy=-1)))
        sweep(half, lambda j: [level6(j), level4(j)])
        arrived(VIA_Z, 1, half)
        send(slots[VIA_Z], R128, 1, half, ZM2, at(dz=-2))
        arrived(VIA_Z, 0, half, LOWER)
        send(slots[VIA_Z], R128, 0, half, ZM2, at(dz=-2), LOWER, 4 + half)

    def near(half):
        for which in range(2):

            def pass_x():
                arrived(VIA_X, which, half)
                send(slots[VIA_X], R16, which, half, XB2, at(dx=-1))

            where(x == 1, pass_x)
            arrived(R2, which, half)
            where(y < 3, lambda: send(slots[R2], R4, which, half, Y2, at(dy=1)))
            where(c == 1, lambda: send(slots[R2], R1, which, half, C1, at(dc=1)))

            def pass_y():
                arrived(VIA_Y, which, half)
                send(slots[VIA_Y], R4, which, half, YB2, at(dy=-1))

            where(y == 1, pass_y)

        for which in range(2):
            arrived(R1, which, half)
        sweep(half, lambda j: [level1(j), level2(j)])

    def far(half):
        arrived(R64, 0, half)
        send(slots[R64], R128, 0, half, ZP, at(dz=2), UPPER)
        arrived(R64, 1, half)
        for which in range(2):
            arrived(R16, which, half)
        sweep(half, lambda j: [level7(j), level5(j)])

    def middle(half):
        for which in range(2):
            arrived(R4, which, half)
        sweep(half, lambda j: [] if j else [(slots[R1], 1, 0), level3(j)])

    late = jnp.where((x == 0) & (y <= 1), 1, 0) if comm else 0

    def stage(i, carry):
        pl.when(i < 2)(lambda: phase1(i))
        pl.when((i == 0) | (i == 1 + late))(lambda: near(jnp.minimum(i, 1)))
        pl.when((i == 2 - late) | (i == 3))(lambda: far(i // 3))
        pl.when(i >= 2)(lambda: middle(i - 2))
        return carry

    lax.fori_loop(0, 4, stage, 0)

    def phase3(half):
        arrived(R128, 0, half, UPPER)
        arrived(R128, 0, half, LOWER, 4 + half)
        arrived(R128, 1, half)
        sweep(half, lambda j: [level8(j)] + [level3(j)] * j, last=True)

    halves(phase3)

    for g in range(KV_HEADS):
        out_copy(g).wait()

    if comm:

        def sent(lane, which, half, rows=(0, 2 * BLOCK), sem=None):
            remote(own, R1, which, half, lane, at(dz=1), rows, sem).wait_send()

        for half in range(2):
            for which in range(2):
                for lane in (Z1, X1, Y1, C1, Z2):
                    sent(lane, which, half)
                for condition, lane in (
                    (x < 3, X2), (x == 2, XB), (x == 1, XB2), (y < 3, Y2), (y == 2, YB), (y == 1, YB2),
                ):
                    where(condition, lambda: sent(lane, which, half))
            for lane in (ZM, ZM2):
                sent(lane, 1, half)
            sent(ZM, 0, half, LOWER)
            sent(ZM2, 0, half, LOWER, 4 + half)
            sent(ZP, 0, half, UPPER)


def copy_kernel(source, target, held, in_sem, out_sem):
    chunks, rows = held.shape[0], held.shape[1]

    def read(i):
        return pltpu.make_async_copy(source.at[pl.ds(i * rows, rows)], held.at[i], in_sem.at[i])

    def write(i):
        return pltpu.make_async_copy(held.at[i], target.at[pl.ds(i * rows, rows)], out_sem.at[i])

    for i in range(chunks):
        read(i).start()
    for i in range(chunks):
        read(i).wait()
        write(i).start()
    for i in range(chunks):
        write(i).wait()


def copied(array):
    rows, width = array.shape
    chunks = 16
    return pl.pallas_call(
        copy_kernel,
        out_shape=jax.ShapeDtypeStruct(array.shape, array.dtype),
        in_specs=[pl.BlockSpec(memory_space=pl.ANY)],
        out_specs=pl.BlockSpec(memory_space=pl.ANY),
        scratch_shapes=[
            pltpu.VMEM((chunks, rows // chunks, width), array.dtype),
            pltpu.SemaphoreType.DMA((chunks,)),
            pltpu.SemaphoreType.DMA((chunks,)),
        ],
        compiler_params=pltpu.CompilerParams(vmem_limit_bytes=63 * 1024 * 1024),
        name="copy_out",
    )(array)


def body(queries, keys, values, pattern, keep, comm=True):
    rows, width = queries.shape
    kv = pltpu.VMEM(keys.shape, keys.dtype)
    result = pl.pallas_call(
        functools.partial(kernel, comm),
        out_shape=jax.ShapeDtypeStruct((rows, width), queries.dtype),
        in_specs=[pl.BlockSpec(memory_space=pl.ANY)] * 5,
        out_specs=pl.BlockSpec(memory_space=pl.ANY),
        scratch_shapes=[kv] * (2 * SLOTS + 2)
        + [
            pltpu.VMEM((rows, width), queries.dtype),
            pltpu.VMEM((rows, width), queries.dtype),
            pltpu.VMEM((rows, width), queries.dtype),
            pltpu.VMEM((2 * KV_HEADS, GROUP * BLOCK, 2 * HEAD), jnp.float32),
            pltpu.VMEM((2 * KV_HEADS, GROUP * BLOCK, HEAD), jnp.float32),
            pltpu.VMEM((pattern.shape[1], HEAD), jnp.int32),
            pltpu.VMEM((keep.shape[1], HEAD), jnp.int32),
            pltpu.VMEM((2 * LEVELS, BLOCK, HEAD), jnp.bfloat16),
            pltpu.VMEM((2 * LEVELS, BLOCK, HEAD), jnp.bfloat16),
            pltpu.VMEM((2 * LEVELS, BLOCK, HEAD), jnp.bfloat16),
            pltpu.SemaphoreType.DMA((5,)),
            pltpu.SemaphoreType.DMA((KV_HEADS,)),
            pltpu.SemaphoreType.DMA((14, PIECES + 2)),
            pltpu.SemaphoreType.DMA((SLOTS, PIECES + 2)),
        ],
        compiler_params=pltpu.CompilerParams(
            vmem_limit_bytes=63 * 1024 * 1024,
            **(dict(collective_id=0, has_side_effects=True) if comm else {}),
        ),
        name="butterfly_attention",
    )(queries, keys, values, pattern.T, keep.T)
    return copied(result)


def solution(mesh):
    return jax.shard_map(
        body,
        mesh=mesh,
        in_specs=(
            P(("seq", "head"), None),
            P(("seq", "head"), None),
            P(("seq", "head"), None),
            P(),
            P(),
        ),
        out_specs=P(("seq", "head"), None),
        check_vma=False,
    )
```

```python
import functools
import math

import jax
import jax.numpy as jnp
from jax import lax
from jax.experimental import pallas as pl
from jax.experimental.pallas import tpu as pltpu
from jax.sharding import PartitionSpec as P

GROUP = 8
KV_HEADS = 8
HEAD = 128
BLOCK = 128
LEVELS = 9
STEEP = math.log2(math.e) / math.sqrt(HEAD)
TILE = 8
WIDE = 2
NEG = -1e30
MESH = pl.DeviceIdType.MESH

R1, R2, R4, R8, R16, R32, R64, R128, VIA_Z, VIA_X, VIA_Y = range(11)
SLOTS = 11
PIECES = 4
HALF = KV_HEADS // 2


def piece_of(pair, which, half, rows=(0, 2 * BLOCK)):
    columns = pl.ds(pl.multiple_of(half * HALF * HEAD, HALF * HEAD), HALF * HEAD)
    return pair[which].at[pl.ds(rows[0], rows[1]), columns]


UPPER, LOWER = (0, 192), (192, 64)


def kernel(comm, q_hbm, k_hbm, v_hbm, pattern_hbm, keep_hbm, out_hbm, *scratch):
    buffers = scratch[: 2 * SLOTS + 2]
    (q, q_rest, out, acc, peak, pattern, keep, first_table, second_table, none_table, load_sem, out_sem, send_sem, recv_sem) = scratch[2 * SLOTS + 2 :]
    own_hbm = (k_hbm, v_hbm)
    own = (buffers[0], buffers[1])
    slots = [(buffers[2 + 2 * i], buffers[3 + 2 * i]) for i in range(SLOTS)]

    if comm:
        s, h = lax.axis_index("seq"), lax.axis_index("head")
    else:
        s, h = jnp.int32(17), jnp.int32(3)
    z, x, y, c = s // 4, s % 4, h // 2, h % 2
    me = s * 8 + h

    def at(dz=0, dx=0, dy=0, dc=0):
        return (
            ((z + dz + 8) % 8) * 4 + (x + dx + 4) % 4,
            ((y + dy + 4) % 4) * 2 + (c + dc) % 2,
        )

    lanes = pl.ds(pl.multiple_of((me // 64) * HEAD, HEAD), HEAD)
    loads = [
        pltpu.make_async_copy(pattern_hbm.at[:, lanes], pattern, load_sem.at[0]),
        pltpu.make_async_copy(keep_hbm.at[:, lanes], keep, load_sem.at[1]),
        pltpu.make_async_copy(k_hbm, own[0], load_sem.at[2]),
        pltpu.make_async_copy(v_hbm, own[1], load_sem.at[3]),
        pltpu.make_async_copy(q_hbm, q, load_sem.at[4]),
    ]
    for load in loads:
        load.start()

    def remote(source, slot, which, half, lane, target, rows=(0, 2 * BLOCK), sem=None):
        piece = 2 * half + which if sem is None else sem
        return pltpu.make_async_remote_copy(
            src_ref=piece_of(source, which, half, rows),
            dst_ref=piece_of(slots[slot], which, half, rows),
            send_sem=send_sem.at[lane, piece],
            recv_sem=recv_sem.at[slot, piece],
            device_id=target,
            device_id_type=MESH,
        )

    def arrived(slot, which, half, rows=(0, 2 * BLOCK), sem=None):
        if comm:
            remote(slots[slot], slot, which, half, 0, at(dz=1), rows, sem).wait_recv()

    Z1, X1, Y1, C1, Z2, X2, XB, XB2, Y2, YB, YB2, ZP, ZM, ZM2 = range(14)

    def send(*args, **kwargs):
        if comm:
            remote(*args, **kwargs).start()

    def where(condition, do):
        if comm:
            pl.when(condition)(do)

    if comm:
        barrier = pltpu.get_barrier_semaphore()
        partners = [
            at(dz=1), at(dz=-1), at(dz=2), at(dz=-2), at(dx=1), at(dx=-1), at(dy=1), at(dy=-1), at(dc=1),
        ]
        for partner in partners:
            pl.semaphore_signal(barrier, inc=1, device_id=partner, device_id_type=MESH)
        pl.semaphore_wait(barrier, len(partners))

        for half in range(2):
            for which in range(2):
                send(own_hbm, R32, which, half, Z1, at(dz=1))
                where(x < 3, lambda: send(own_hbm, R8, which, half, X1, at(dx=1)))
                where(y < 3, lambda: send(own_hbm, R2, which, half, Y1, at(dy=1)))
                where(c == 0, lambda: send(own_hbm, R1, which, half, C1, at(dc=1)))
            send(own_hbm, VIA_Z, 1, half, ZM, at(dz=-2))
            send(own_hbm, VIA_Z, 0, half, ZM, at(dz=-2), LOWER)

    for load in loads:
        load.wait()

    line = lax.broadcasted_iota(jnp.int32, pattern.shape, 0)
    column = lax.broadcasted_iota(jnp.int32, pattern.shape, 1)
    blocks, kept = pattern[...].astype(jnp.float32), keep[...].astype(jnp.float32)
    for j in range(2):
        for level in range(LEVELS):
            here = (line == level) & (column == (me % 64) * 2 + j)

            def entry(table):
                found = jnp.where(here, table, 0.0)
                return jnp.sum(jnp.sum(found, axis=1, keepdims=True), axis=0, keepdims=True)

            base = (2 * (me - max(1, 2**level // 2))).astype(jnp.float32)
            second = jnp.clip(entry(blocks) - base, 0.0, 1.0)
            used = entry(kept)
            if level == 0:
                second = jnp.zeros_like(second)
            for table, value in (
                (first_table, used * (1.0 - second)), (second_table, used * second), (none_table, 1.0 - used),
            ):
                table[j * LEVELS + level] = jnp.broadcast_to(value, (BLOCK, HEAD)).astype(jnp.bfloat16)

    def queries_of(item, first):
        j, g, t = item
        rows = pl.ds(j * BLOCK, BLOCK)
        found = []
        for r in range(TILE):
            columns = pl.ds(pl.multiple_of((g * GROUP + t * TILE + r) * HEAD, HEAD), HEAD)
            if first:
                scaled = q[rows, columns].astype(jnp.float32) * STEEP
                whole = scaled.astype(jnp.bfloat16)
                rest = (scaled - whole.astype(jnp.float32)).astype(jnp.bfloat16)
                q[rows, columns], q_rest[rows, columns] = whole, rest
            else:
                whole, rest = q[rows, columns], q_rest[rows, columns]
            found.append(jnp.concatenate([whole, rest], 1))
        return jnp.concatenate(found, 0) if TILE > 1 else found[0]

    def gathered(j, g, sources):
        columns = pl.ds(pl.multiple_of(g * HEAD, HEAD), HEAD)

        anchor = jnp.broadcast_to(own[0][pl.ds(j * BLOCK, 1), columns], (BLOCK, HEAD))
        keys, values = [], []
        for pair, block, level in sources:
            key, value = (
                [ref[pl.ds(i * BLOCK, BLOCK), columns] for i in (range(2) if block is None else (block,))]
                for ref in pair
            )
            if level is None:
                keys.append(key[0])
                values.append(jnp.concatenate([value[0], jnp.ones_like(value[0])], 1))
                continue
            table = j * LEVELS + level
            one, none = first_table[table], none_table[table]
            total_key, total_value = key[0] * one + anchor * none, value[0] * one
            ones = one
            if block is None:
                two = second_table[table]
                total_key, total_value = total_key + key[1] * two, total_value + value[1] * two
                ones = one + two
            keys.append(total_key)
            values.append(jnp.concatenate([total_value, ones], 1))
        keys = jnp.concatenate(keys, 0) if len(keys) > 1 else keys[0]
        values = jnp.concatenate(values, 0) if len(values) > 1 else values[0]
        return jnp.concatenate([keys, keys], 1), values

    def scores_of(item, keys, first):
        return lax.dot_general(
            queries_of(item, first), keys, (((1,), (1,)), ((), ())),
            preferred_element_type=jnp.float32,
        )

    def finish(item, scores, values, levels, first, last):
        j, g, t = item
        unit = g * 2 + j
        tile = pl.ds(t * TILE * BLOCK, TILE * BLOCK)
        parts = []
        for i, level in enumerate(levels):
            part = scores[:, i * BLOCK : (i + 1) * BLOCK]
            if level is None:
                token = lax.broadcasted_iota(jnp.int32, part.shape, 0) % BLOCK
                key = lax.broadcasted_iota(jnp.int32, part.shape, 1)
                part = jnp.where(key <= token, part, NEG)
            parts.append(part)
        top = functools.reduce(jnp.maximum, parts)
        top = jnp.max(top, axis=1, keepdims=True)
        top = jnp.broadcast_to(top, (TILE * BLOCK, HEAD))
        if not first:
            before = peak[unit, tile]
            top = jnp.maximum(before, top)
        weights = [jnp.exp2(part - top).astype(jnp.bfloat16) for part in parts]
        weights = jnp.concatenate(weights, 1) if len(weights) > 1 else weights[0]
        total = jnp.dot(weights, values, preferred_element_type=jnp.float32)
        if not first:
            fade = jnp.exp2(before - top)
            total = total + acc[unit, tile] * jnp.concatenate([fade, fade], 1)
        if last:
            result = (total[:, :HEAD] / total[:, HEAD:]).astype(jnp.bfloat16)
            for r in range(TILE):
                columns = pl.ds(pl.multiple_of((g * GROUP + t * TILE + r) * HEAD, HEAD), HEAD)
                out[pl.ds(j * BLOCK, BLOCK), columns] = result[r * BLOCK : (r + 1) * BLOCK]
        else:
            acc[unit, tile] = total
            peak[unit, tile] = top

    def out_copy(g):
        columns = pl.ds(pl.multiple_of(g * GROUP * HEAD, HEAD), GROUP * HEAD)
        return pltpu.make_async_copy(out.at[:, columns], out_hbm.at[:, columns], out_sem.at[g])

    def sweep(half, sources_of, first=False, last=False):
        def step(i, carry):
            waiting = None
            for g in range(WIDE):
                g = half * HALF + i * WIDE + g
                for j in range(2):
                    sources = sources_of(j)
                    if not sources:
                        continue
                    keys, values = gathered(j, g, sources)
                    levels = [level for _, _, level in sources]
                    for t in range(GROUP // TILE):
                        item = (j, g, t)
                        scores = scores_of(item, keys, first)
                        if waiting is not None:
                            finish(*waiting, first, last)
                        waiting = (item, scores, values, levels)
            finish(*waiting, first, last)
            if last:
                for g in range(WIDE):
                    out_copy(half * HALF + i * WIDE + g).start()
            return carry

        lax.fori_loop(0, HALF // WIDE, step, 0)

    def level_source(level, slot):
        return lambda j: (slots[slot], None, level)

    level1, level2 = level_source(1, R1), level_source(2, R2)
    level3, level4 = level_source(3, R4), level_source(4, R8)
    level5, level6 = level_source(5, R16), level_source(6, R32)
    level7, level8 = level_source(7, R64), level_source(8, R128)

    def halves(phase):
        def step(half, carry):
            phase(half)
            return carry

        lax.fori_loop(0, 2, step, 0)

    def diagonal(j):
        return [(own, j, None)] + [(own, 0, 0)] * j

    halves(lambda half: sweep(half, diagonal, first=True))

    def phase1(half):
        for which in range(2):
            arrived(R32, which, half)
            send(slots[R32], R64, which, half, Z2, at(dz=1))
            where(x == 3, lambda: send(slots[R32], R8, which, half, X1, at(dx=1)))
            where(x == 2, lambda: send(slots[R32], VIA_X, which, half, XB, at(dx=-1)))
            arrived(R8, which, half)
            where(x < 3, lambda: send(slots[R8], R16, which, half, X2, at(dx=1)))
            where(y == 3, lambda: send(slots[R8], R2, which, half, Y1, at(dy=1)))
            where(y == 2, lambda: send(slots[R8], VIA_Y, which, half, YB, at(dy=-1)))
        sweep(half, lambda j: [level6(j), level4(j)])
        arrived(VIA_Z, 1, half)
        send(slots[VIA_Z], R128, 1, half, ZM2, at(dz=-2))
        arrived(VIA_Z, 0, half, LOWER)
        send(slots[VIA_Z], R128, 0, half, ZM2, at(dz=-2), LOWER, 4 + half)

    def near(half):
        for which in range(2):

            def pass_x():
                arrived(VIA_X, which, half)
                send(slots[VIA_X], R16, which, half, XB2, at(dx=-1))

            where(x == 1, pass_x)
            arrived(R2, which, half)
            where(y < 3, lambda: send(slots[R2], R4, which, half, Y2, at(dy=1)))
            where(c == 1, lambda: send(slots[R2], R1, which, half, C1, at(dc=1)))

            def pass_y():
                arrived(VIA_Y, which, half)
                send(slots[VIA_Y], R4, which, half, YB2, at(dy=-1))

            where(y == 1, pass_y)

        for which in range(2):
            arrived(R1, which, half)
        sweep(half, lambda j: [level1(j), level2(j)])

    def far(half):
        arrived(R64, 0, half)
        send(slots[R64], R128, 0, half, ZP, at(dz=2), UPPER)
        arrived(R64, 1, half)
        for which in range(2):
            arrived(R16, which, half)
        sweep(half, lambda j: [level7(j), level5(j)])

    def middle(half):
        for which in range(2):
            arrived(R4, which, half)
        sweep(half, lambda j: [] if j else [(slots[R1], 1, 0), level3(j)])

    late = jnp.where((x == 0) & (y <= 1), 1, 0) if comm else 0

    def stage(i, carry):
        pl.when(i < 2)(lambda: phase1(i))
        pl.when((i == 0) | (i == 1 + late))(lambda: near(jnp.minimum(i, 1)))
        pl.when((i == 2 - late) | (i == 3))(lambda: far(i // 3))
        pl.when(i >= 2)(lambda: middle(i - 2))
        return carry

    lax.fori_loop(0, 4, stage, 0)

    def phase3(half):
        arrived(R128, 0, half, UPPER)
        arrived(R128, 0, half, LOWER, 4 + half)
        arrived(R128, 1, half)
        sweep(half, lambda j: [level8(j)] + [level3(j)] * j, last=True)

    halves(phase3)

    for g in range(KV_HEADS):
        out_copy(g).wait()

    if comm:

        def sent(lane, which, half, rows=(0, 2 * BLOCK), sem=None):
            remote(own, R1, which, half, lane, at(dz=1), rows, sem).wait_send()

        for half in range(2):
            for which in range(2):
                for lane in (Z1, X1, Y1, C1, Z2):
                    sent(lane, which, half)
                for condition, lane in (
                    (x < 3, X2), (x == 2, XB), (x == 1, XB2), (y < 3, Y2), (y == 2, YB), (y == 1, YB2),
                ):
                    where(condition, lambda: sent(lane, which, half))
            for lane in (ZM, ZM2):
                sent(lane, 1, half)
            sent(ZM, 0, half, LOWER)
            sent(ZM2, 0, half, LOWER, 4 + half)
            sent(ZP, 0, half, UPPER)


def copy_kernel(source, target, held, in_sem, out_sem):
    chunks, rows = held.shape[0], held.shape[1]

    def read(i):
        return pltpu.make_async_copy(source.at[pl.ds(i * rows, rows)], held.at[i], in_sem.at[i])

    def write(i):
        return pltpu.make_async_copy(held.at[i], target.at[pl.ds(i * rows, rows)], out_sem.at[i])

    for i in range(chunks):
        read(i).start()
    for i in range(chunks):
        read(i).wait()
        write(i).start()
    for i in range(chunks):
        write(i).wait()


def copied(array):
    rows, width = array.shape
    chunks = 16
    return pl.pallas_call(
        copy_kernel,
        out_shape=jax.ShapeDtypeStruct(array.shape, array.dtype),
        in_specs=[pl.BlockSpec(memory_space=pl.ANY)],
        out_specs=pl.BlockSpec(memory_space=pl.ANY),
        scratch_shapes=[
            pltpu.VMEM((chunks, rows // chunks, width), array.dtype),
            pltpu.SemaphoreType.DMA((chunks,)),
            pltpu.SemaphoreType.DMA((chunks,)),
        ],
        compiler_params=pltpu.CompilerParams(vmem_limit_bytes=63 * 1024 * 1024),
        name="copy_out",
    )(array)


def body(queries, keys, values, pattern, keep, comm=True):
    rows, width = queries.shape
    kv = pltpu.VMEM(keys.shape, keys.dtype)
    result = pl.pallas_call(
        functools.partial(kernel, comm),
        out_shape=jax.ShapeDtypeStruct((rows, width), queries.dtype),
        in_specs=[pl.BlockSpec(memory_space=pl.ANY)] * 5,
        out_specs=pl.BlockSpec(memory_space=pl.ANY),
        scratch_shapes=[kv] * (2 * SLOTS + 2)
        + [
            pltpu.VMEM((rows, width), queries.dtype),
            pltpu.VMEM((rows, width), queries.dtype),
            pltpu.VMEM((rows, width), queries.dtype),
            pltpu.VMEM((2 * KV_HEADS, GROUP * BLOCK, 2 * HEAD), jnp.float32),
            pltpu.VMEM((2 * KV_HEADS, GROUP * BLOCK, HEAD), jnp.float32),
            pltpu.VMEM((pattern.shape[1], HEAD), jnp.int32),
            pltpu.VMEM((keep.shape[1], HEAD), jnp.int32),
            pltpu.VMEM((2 * LEVELS, BLOCK, HEAD), jnp.bfloat16),
            pltpu.VMEM((2 * LEVELS, BLOCK, HEAD), jnp.bfloat16),
            pltpu.VMEM((2 * LEVELS, BLOCK, HEAD), jnp.bfloat16),
            pltpu.SemaphoreType.DMA((5,)),
            pltpu.SemaphoreType.DMA((KV_HEADS,)),
            pltpu.SemaphoreType.DMA((14, PIECES + 2)),
            pltpu.SemaphoreType.DMA((SLOTS, PIECES + 2)),
        ],
        compiler_params=pltpu.CompilerParams(
            vmem_limit_bytes=63 * 1024 * 1024,
            **(dict(collective_id=0, has_side_effects=True) if comm else {}),
        ),
        name="butterfly_attention",
    )(queries, keys, values, pattern.T, keep.T)
    return copied(result)


def solution(mesh):
    return jax.shard_map(
        body,
        mesh=mesh,
        in_specs=(
            P(("seq", "head"), None),
            P(("seq", "head"), None),
            P(("seq", "head"), None),
            P(),
            P(),
        ),
        out_specs=P(("seq", "head"), None),
        check_vma=False,
    )
```
